32 devices in a mesh: blk: 8 (over z, y), grp: 4 (over x, core).
Axes of the slice: x: 2, y: 2, z: 4, core: 2. Of those that a mesh axis runs over, the one named last changes fastest.
Arguments:
- tables: float32 [8, 8192, 128], P('grp', 'blk'), may hold values from -1 to 1
- bag_ids: int32 [1024, 8, 32], P('blk', 'grp'), may hold values from 0 to 8191, as said below
Outputs:
- pooled: float32 [1024, 8, 128], P('blk', 'grp')
- interaction: float32 [1024, 8, 8], P('blk', 'grp')
The draws below stay inside these ranges and needn't reach their ends.
Inputs may be any that keep to these rules, and one draw needn't show every extreme that they name: `bag_ids`: some rows are far more popular than others.
All inputs are finite; a program needn't handle non-finite values.
Results may differ from the reference program's by a relative error of at most 0.000065.
Values sent between devices are 32-bit elements; how exact they have to be, the bound alone decides.
A program may use at most 64 MiB of HBM per device.

```python
import math
import jax
import jax.numpy as jnp
from jax import lax

E = 128
ROWS_DEV = 1024
BAG = 32
SECTIONS = 8
B_DEV = 128
ROWS = 8192
TABLES = 8
BATCH = 1024
N_BLK = 8


def draw_bag_ids(key, part):
    subkeys = jax.random.split(key, 5)
    id_shape = (BATCH, TABLES, BAG)
    distance = jax.random.randint(subkeys[0], id_shape, 0, SECTIONS)
    uniform_rows = jax.random.randint(subkeys[1], id_shape, 0, ROWS_DEV)
    hot_table = jax.random.randint(subkeys[2], (TABLES, 16), 0, ROWS_DEV)
    hot_pick = jax.random.randint(subkeys[3], id_shape, 0, 16)
    hot_rows = hot_table[jnp.arange(TABLES, dtype=jnp.int32)[None, :, None], hot_pick]
    popular = jax.random.randint(subkeys[4], id_shape, 0, 3) == 0
    row_choice = jnp.where(popular, hot_rows, uniform_rows)
    return (row_choice * SECTIONS + distance).astype(jnp.int32)


def levels(own_key, shape, cuts, least, top_value):
    loudness, own = 1.0, jax.random.fold_in(own_key, 6)
    for axis_at, parts in cuts:
        heights = jnp.exp(jax.random.uniform(jax.random.fold_in(own, axis_at), (parts,), jnp.float32, least / len(cuts), top_value / len(cuts)))
        loudness = loudness * jnp.repeat(heights, shape[axis_at] // parts).reshape([-1 if axis == axis_at else 1 for axis in range(len(shape))])
    return loudness


def scatter_about(rng, shape, deviation, most, pieces=(), kind=jnp.bfloat16):
    gain = levels(rng, shape, pieces, -0.22, 0.18) if pieces else 1.0
    entries = jax.random.normal(rng, shape, jnp.float32) * deviation * gain
    return jnp.minimum(jnp.maximum(entries, -most), most).astype(kind)


def setup_inputs(seed: int = 0) -> dict:
    keys = jax.random.split(jax.random.key(seed), 3)
    return {
        "tables": scatter_about(keys[0], (TABLES, ROWS, E), 0.18, 1.0, ((0, 4), (1, 8)), jnp.float32),
        "bag_ids": draw_bag_ids(jax.random.fold_in(keys[2], 71), 0),
    }


def reference(tables, bag_ids):
    home_shard = (jnp.arange(BATCH, dtype=jnp.int32) // B_DEV)[:, None, None]
    distance = bag_ids % SECTIONS
    local_row = bag_ids // SECTIONS
    row_index = (((home_shard - distance) % N_BLK) * ROWS_DEV + local_row).astype(jnp.int32)
    block_size = math.gcd(BATCH, 512)
    grouped = row_index.reshape(BATCH // block_size, block_size, TABLES, BAG)

    def one_block(block_ids):
        columns = [jnp.sum(tables[table_num][block_ids[:, table_num, :]], axis=1) for table_num in range(TABLES)]
        return jnp.stack(columns, axis=1)

    pooled = lax.map(one_block, grouped).reshape(BATCH, TABLES, E)
    interaction = jnp.einsum("bte,bue->btu", pooled, pooled, precision=lax.Precision.HIGHEST) / E
    return pooled, interaction
```

```python
import functools

import jax
import jax.numpy as jnp
from jax import lax
from jax.experimental import pallas as pl
from jax.experimental.pallas import tpu as pltpu
from jax.sharding import PartitionSpec as P

SECTIONS = 8
MESH = pl.DeviceIdType.MESH
VMEM = pl.BlockSpec(memory_space=pltpu.VMEM)
CHUNK = 256
FAR = 1 << 20


def gather_ids_kernel(n, ids_ref, out_ref, send_sem, recv_sem):
    me = lax.axis_index("blk")
    rows = ids_ref.shape[0]
    barrier = pltpu.get_barrier_semaphore()
    count = 0
    for d in range(1, SECTIONS):
        pl.semaphore_signal(barrier, inc=1, device_id={"blk": lax.rem(me + d, n)}, device_id_type=MESH)
        count += 1
        if n != SECTIONS:
            pl.semaphore_signal(barrier, inc=1, device_id={"blk": lax.rem(me + n - d, n)}, device_id_type=MESH)
            count += 1
    pl.semaphore_wait(barrier, count)
    copies = []
    for d in range(1, SECTIONS):
        copy = pltpu.make_async_remote_copy(
            src_ref=ids_ref,
            dst_ref=out_ref.at[pl.ds(d * rows, rows)],
            send_sem=send_sem.at[d - 1],
            recv_sem=recv_sem.at[d - 1],
            device_id={"blk": lax.rem(me + n - d, n)},
            device_id_type=MESH,
        )
        copy.start()
        copies.append(copy)
    out_ref[pl.ds(0, rows)] = ids_ref[...]
    for copy in copies:
        copy.wait()


def gather_ids(n, ids):
    rows, lanes = ids.shape
    return pl.pallas_call(
        functools.partial(gather_ids_kernel, n),
        out_shape=jax.ShapeDtypeStruct((SECTIONS * rows, lanes), jnp.int32),
        in_specs=[VMEM],
        out_specs=VMEM,
        scratch_shapes=[
            pltpu.SemaphoreType.DMA((SECTIONS - 1,)),
            pltpu.SemaphoreType.DMA((SECTIONS - 1,)),
        ],
        compiler_params=pltpu.CompilerParams(collective_id=0, has_side_effects=True),
        name="gather_ids",
    )(ids)


def bitonic_merge(x):
    half = len(x) // 2
    if half == 0:
        return x
    low = [jnp.minimum(x[i], x[i + half]) for i in range(half)]
    high = [jnp.maximum(x[i], x[i + half]) for i in range(half)]
    return bitonic_merge(low) + bitonic_merge(high)


def bitonic_sort(x):
    if len(x) == 1:
        return x
    half = len(x) // 2
    return bitonic_merge(bitonic_sort(x[:half]) + bitonic_sort(x[half:])[::-1])


def pool_kernel(bag, ids_ref, table_ref, part_ref, keys, counts, table_t):
    tables, rows, width = table_ref.shape
    groups = ids_ref.shape[0] // bag
    lanes = ids_ref.shape[1]
    chunks = rows // CHUNK
    for t in range(tables):
        whole = table_ref[t]
        flipped = whole.T
        high = flipped.astype(jnp.bfloat16)
        table_t[t, pl.ds(0, width), :] = high
        table_t[t, pl.ds(width, width), :] = (flipped - high.astype(jnp.float32)).astype(jnp.bfloat16)
    section = lax.broadcasted_iota(jnp.int32, (groups, lanes), 0) // tables
    entries = []
    for p in range(bag):
        code = ids_ref[pl.ds(p, groups, stride=bag), :]
        entries.append(jnp.where((code & (SECTIONS - 1)) == section, code >> 3, FAR))
    entries = bitonic_sort(entries)
    pairs = SECTIONS // 2
    trips = []
    for c in range(chunks):
        inside = [
            jnp.where((x >= c * CHUNK) & (x < (c + 1) * CHUNK), x - c * CHUNK, FAR) for x in entries
        ]
        inside = bitonic_merge(inside)
        used = jnp.zeros((groups, lanes), jnp.int32)
        for p in range(bag):
            used = used + (inside[p] < FAR).astype(jnp.int32)
            keys[c, p] = inside[p].astype(jnp.float32)
        step = groups // pairs
        trips.append([jnp.max(used[q * step : (q + 1) * step]) for q in range(pairs)])
    index = lax.broadcasted_iota(jnp.int32, (CHUNK, lanes), 0).astype(jnp.float32).astype(jnp.bfloat16)
    one, zero = jnp.bfloat16(1), jnp.bfloat16(0)
    for t in range(tables):
        for c in range(chunks):
            for q in range(pairs):
                places = [(2 * q) * tables + t, (2 * q + 1) * tables + t]

                def body(j, acc):
                    fresh = []
                    for place, total in zip(places, acc):
                        key = keys[c, j, pl.ds(place, 1), :]
                        key = jnp.broadcast_to(key, (CHUNK, lanes)).astype(jnp.bfloat16)
                        fresh.append(total + jnp.where(index == key, one, zero))
                    return tuple(fresh)

                empty = jnp.zeros((CHUNK, lanes), jnp.bfloat16)
                acc = lax.fori_loop(0, trips[c][q], body, (empty, empty))
                for i in range(2):
                    counts[pl.ds(c * CHUNK, CHUNK), pl.ds((2 * q + i) * lanes, lanes)] = acc[i]
        for q in range(pairs):
            total = jnp.dot(
                table_t[t], counts[:, pl.ds(2 * q * lanes, 2 * lanes)], preferred_element_type=jnp.float32
            )
            total = total[:width] + total[width:]
            for i in range(2):
                part_ref[2 * q + i, t] = total[:, i * lanes : (i + 1) * lanes]


def pool(bag, ids, tables):
    count, rows, width = tables.shape
    lanes = ids.shape[1]
    groups = ids.shape[0] // bag
    return pl.pallas_call(
        functools.partial(pool_kernel, bag),
        out_shape=jax.ShapeDtypeStruct((SECTIONS, count, width, lanes), jnp.float32),
        in_specs=[VMEM, VMEM],
        out_specs=VMEM,
        scratch_shapes=[
            pltpu.VMEM((rows // CHUNK, bag, groups, lanes), jnp.float32),
            pltpu.VMEM((rows, SECTIONS * lanes), jnp.bfloat16),
            pltpu.VMEM((count, 2 * width, rows), jnp.bfloat16),
        ],
        name="pool",
    )(ids, tables)


PIECES = 2


def finish_kernel(n, groups, part_ref, pooled_ref, inter_ref, held, mixed, gram, grams, *sems):
    ring_send, ring_recv, mix_send, mix_recv, gram_send, gram_recv = sems
    sections, tables, width, lanes = part_ref.shape
    me, grp = lax.axis_index("blk"), lax.axis_index("grp")
    last = sections - 1
    piece = width // PIECES
    quarter = width // groups
    whole_ring = n == sections

    if whole_ring:
        place = jnp.where(me % 2 == 0, me // 2, n - 1 - me // 2)
        ways = [1 if t % 2 == 0 else n - 1 for t in range(tables)]
    else:
        place = me
        ways = [1 for t in range(tables)]

    def at(position):
        position = lax.rem(position, n)
        if whole_ring:
            return jnp.where(position < n // 2, 2 * position, 2 * (n - 1 - position) + 1)
        return position

    def section_of(t, away):
        return lax.rem(at(place + ways[t] * away) + n - me, n)

    barrier = pltpu.get_barrier_semaphore()
    for neighbour in (at(place + 1), at(place + n - 1)):
        pl.semaphore_signal(barrier, inc=1, device_id={"blk": neighbour}, device_id_type=MESH)
    for k in range(1, groups):
        pl.semaphore_signal(barrier, inc=1, device_id={"grp": lax.rem(grp + k, groups)}, device_id_type=MESH)
    pl.semaphore_wait(barrier, 2 + groups - 1)

    def hop(step, t, c, source):
        return pltpu.make_async_remote_copy(
            src_ref=source,
            dst_ref=held.at[step, t, pl.ds(c * piece, piece)],
            send_sem=ring_send.at[step, t, c],
            recv_sem=ring_recv.at[step, t, c],
            device_id={"blk": at(place + ways[t])},
            device_id_type=MESH,
        )

    flying = {}
    for c in range(PIECES):
        for t in range(tables):
            flying[0, t, c] = hop(0, t, c, part_ref.at[section_of(t, last), t, pl.ds(c * piece, piece)])
            flying[0, t, c].start()
    for step in range(last):
        for c in range(PIECES):
            for t in range(tables):
                rows = pl.ds(c * piece, piece)
                flying[step, t, c].wait_recv()
                total = held[step, t, rows] + part_ref[section_of(t, last - 1 - step), t, rows]
                if step + 1 < last:
                    held[step, t, rows] = total
                    flying[step + 1, t, c] = hop(step + 1, t, c, held.at[step, t, rows])
                    flying[step + 1, t, c].start()
                else:
                    pooled_ref[t, rows] = total

    mixes = []
    for k in range(1, groups):
        peer = lax.rem(grp + k, groups)
        mixes.append(
            pltpu.make_async_remote_copy(
                src_ref=pooled_ref.at[:, pl.ds(pl.multiple_of(peer * quarter, quarter), quarter)],
                dst_ref=mixed.at[grp],
                send_sem=mix_send.at[k - 1],
                recv_sem=mix_recv.at[k - 1],
                device_id={"grp": peer},
                device_id_type=MESH,
            )
        )
        mixes[-1].start()
    mixed[grp] = pooled_ref[:, pl.ds(pl.multiple_of(grp * quarter, quarter), quarter)]
    for copy in flying.values():
        copy.wait_send()
    for copy in mixes:
        copy.wait_recv()
    every = [mixed[g, t] for g in range(groups) for t in range(tables)]
    scale = 1.0 / width
    for a in range(len(every)):
        for b in range(a, len(every)):
            row = jnp.sum(every[a] * every[b], axis=0, keepdims=True) * scale
            for x, y in {(a, b), (b, a)} if a != b else {(a, b)}:
                gram[x // tables, pl.ds((x % tables) * len(every) + y, 1), :] = row
    sums = []
    for k in range(1, groups):
        peer = lax.rem(grp + k, groups)
        sums.append(
            pltpu.make_async_remote_copy(
                src_ref=gram.at[peer],
                dst_ref=grams.at[k - 1],
                send_sem=gram_send.at[k - 1],
                recv_sem=gram_recv.at[k - 1],
                device_id={"grp": peer},
                device_id_type=MESH,
            )
        )
        sums[-1].start()
    total = gram[grp]
    for k in range(groups - 1):
        sums[k].wait_recv()
        total = total + grams[k]
    inter_ref[...] = total
    for copy in mixes + sums:
        copy.wait_send()


def finish(n, groups, part):
    sections, tables, width, lanes = part.shape
    pairs = tables * tables * groups
    dma = pltpu.SemaphoreType.DMA
    return pl.pallas_call(
        functools.partial(finish_kernel, n, groups),
        out_shape=(
            jax.ShapeDtypeStruct((tables, width, lanes), jnp.float32),
            jax.ShapeDtypeStruct((pairs, lanes), jnp.float32),
        ),
        in_specs=[VMEM],
        out_specs=(VMEM, VMEM),
        scratch_shapes=[
            pltpu.VMEM((sections - 1, tables, width, lanes), jnp.float32),
            pltpu.VMEM((groups, tables, width // groups, lanes), jnp.float32),
            pltpu.VMEM((groups, pairs, lanes), jnp.float32),
            pltpu.VMEM((groups - 1, pairs, lanes), jnp.float32),
            dma((sections - 1, tables, PIECES)),
            dma((sections - 1, tables, PIECES)),
            dma((groups - 1,)),
            dma((groups - 1,)),
            dma((groups - 1,)),
            dma((groups - 1,)),
        ],
        compiler_params=pltpu.CompilerParams(collective_id=1, has_side_effects=True),
        name="finish",
    )(part)


def solution(mesh):
    n, groups = mesh.shape["blk"], mesh.shape["grp"]

    def shards(tables, bag_ids):
        samples, count, bag = bag_ids.shape
        ids = bag_ids.transpose(1, 2, 0).reshape(count * bag, samples)
        ids = gather_ids(n, ids)
        part = pool(bag, ids, tables)
        pooled, inter = finish(n, groups, part)
        pooled = pooled.transpose(2, 0, 1)
        inter = inter.reshape(count, count * groups, samples).transpose(2, 0, 1)
        return pooled, inter

    return jax.shard_map(
        shards,
        mesh=mesh,
        in_specs=(P("grp", "blk", None), P("blk", "grp", None)),
        out_specs=(P("blk", "grp", None), P("blk", "grp", None)),
        check_vma=False,
    )
```

```python
import functools

import jax
import jax.numpy as jnp
from jax import lax
from jax.experimental import pallas as pl
from jax.experimental.pallas import tpu as pltpu
from jax.sharding import PartitionSpec as P

SECTIONS = 8
MESH = pl.DeviceIdType.MESH
VMEM = pl.BlockSpec(memory_space=pltpu.VMEM)
CHUNK = 256


def plan(n, tables):
    if n == SECTIONS:
        far, near = n // 2, n - 1 - n // 2
        chains = {}
        for t in range(tables):
            chains[t, 1] = far if t % 2 == 0 else near
            chains[t, -1] = near if t % 2 == 0 else far
        offsets = [far]
        for k in range(near, 0, -1):
            offsets += [k, -k]
        return chains, offsets + [0]
    chains = {(t, 1): SECTIONS - 1 for t in range(tables)}
    return chains, list(range(SECTIONS - 1, -1, -1))


def kernel(n, groups, bag, ids_ref, table_ref, pooled_ref, inter_ref, *scratch):
    near_ids, table_t, keys, counts, sums, held, mixed, gram, grams, *sems = scratch
    ids_send, ids_recv, ring_send, ring_recv, mix_send, mix_recv, gram_send, gram_recv = sems
    tables, rows, width = table_ref.shape
    lanes = ids_ref.shape[1]
    chunks = rows // CHUNK
    quarter = width // groups
    me, grp = lax.axis_index("blk"), lax.axis_index("grp")
    chains, offsets = plan(n, tables)
    order = list(chains)

    if n == SECTIONS:
        place = jnp.where(me % 2 == 0, me // 2, n - 1 - me // 2)
    else:
        place = me

    def at(offset):
        position = lax.rem(place + offset + n, n)
        if n == SECTIONS:
            return jnp.where(position < n // 2, 2 * position, 2 * (n - 1 - position) + 1)
        return position

    barrier = pltpu.get_barrier_semaphore()
    greeted = 0
    for offset in offsets[:-1]:
        pl.semaphore_signal(barrier, inc=1, device_id={"blk": at(offset)}, device_id_type=MESH)
        greeted += 1
        if n != SECTIONS:
            pl.semaphore_signal(barrier, inc=1, device_id={"blk": at(-offset)}, device_id_type=MESH)
            greeted += 1
    for k in range(1, groups):
        pl.semaphore_signal(barrier, inc=1, device_id={"grp": lax.rem(grp + k, groups)}, device_id_type=MESH)
    pl.semaphore_wait(barrier, greeted + groups - 1)

    asks = []
    for job, offset in enumerate(offsets[:-1]):
        asks.append(
            pltpu.make_async_remote_copy(
                src_ref=ids_ref,
                dst_ref=near_ids.at[job],
                send_sem=ids_send.at[job],
                recv_sem=ids_recv.at[job],
                device_id={"blk": at(-offset)},
                device_id_type=MESH,
            )
        )
        asks[-1].start()

    for t in range(tables):
        flipped = table_ref[t].T
        high = flipped.astype(jnp.bfloat16)
        table_t[t, pl.ds(0, width), :] = high
        table_t[t, pl.ds(width, width), :] = (flipped - high.astype(jnp.float32)).astype(jnp.bfloat16)
    index = lax.broadcasted_iota(jnp.int32, (CHUNK, lanes), 0).astype(jnp.float32).astype(jnp.bfloat16)
    one, zero = jnp.bfloat16(1), jnp.bfloat16(0)

    def partial_sums(codes, section):
        local = jnp.where((codes & (SECTIONS - 1)) == section, codes >> 3, -1)
        for c in range(chunks):
            inside = (local >= c * CHUNK) & (local < (c + 1) * CHUNK)
            keys[c] = jnp.where(inside, local - c * CHUNK, 2 * CHUNK).astype(jnp.float32)

        def unit(u, carry):
            t, c = u // chunks, u % chunks
            total = jnp.zeros((CHUNK, lanes), jnp.bfloat16)
            for p in range(bag):
                key = jnp.broadcast_to(keys[c, pl.ds(t * bag + p, 1), :], (CHUNK, lanes))
                total = total + jnp.where(index == key.astype(jnp.bfloat16), one, zero)
            counts[t, pl.ds(pl.multiple_of(c * CHUNK, CHUNK), CHUNK), :] = total
            return carry

        lax.fori_loop(0, tables * chunks, unit, 0)
        result = []
        for t in range(tables):
            both = jnp.dot(table_t[t], counts[t], preferred_element_type=jnp.float32)
            result.append(both[:width] + both[width:])
        return result

    flying = {}
    for job, offset in enumerate(offsets):
        if offset == 0:
            codes = ids_ref[...]
        else:
            asks[job].wait_recv()
            codes = near_ids[job]
        mine = partial_sums(codes, lax.rem(at(offset) + n - me, n))
        for t, way in order:
            slot, hops = order.index((t, way)), chains[t, way]
            away = hops - offset * way % n
            if offset == 0 or away < 0:
                continue
            total = mine[t]
            if away > 0:
                flying[slot, away - 1].wait_recv()
                total = total + held[slot, away - 1]
            sums[slot, away] = total
            flying[slot, away] = pltpu.make_async_remote_copy(
                src_ref=sums.at[slot, away],
                dst_ref=held.at[slot, away],
                send_sem=ring_send.at[slot, away],
                recv_sem=ring_recv.at[slot, away],
                device_id={"blk": at(way)},
                device_id_type=MESH,
            )
            flying[slot, away].start()
    for t, way in order:
        slot, hops = order.index((t, way)), chains[t, way]
        flying[slot, hops - 1].wait_recv()
        mine[t] = mine[t] + held[slot, hops - 1]
    for t in range(tables):
        pooled_ref[t] = mine[t]

    mixes = []
    for k in range(1, groups):
        peer = lax.rem(grp + k, groups)
        mixes.append(
            pltpu.make_async_remote_copy(
                src_ref=pooled_ref.at[:, pl.ds(pl.multiple_of(peer * quarter, quarter), quarter)],
                dst_ref=mixed.at[grp],
                send_sem=mix_send.at[k - 1],
                recv_sem=mix_recv.at[k - 1],
                device_id={"grp": peer},
                device_id_type=MESH,
            )
        )
        mixes[-1].start()
    mixed[grp] = pooled_ref[:, pl.ds(pl.multiple_of(grp * quarter, quarter), quarter)]
    for copy in list(flying.values()) + asks:
        copy.wait_send()
    for copy in mixes:
        copy.wait_recv()
    every = [mixed[g, t] for g in range(groups) for t in range(tables)]
    for a in range(len(every)):
        for b in range(a, len(every)):
            row = jnp.sum(every[a] * every[b], axis=0, keepdims=True) / width
            gram[a // tables, pl.ds((a % tables) * len(every) + b, 1), :] = row
            if a != b:
                gram[b // tables, pl.ds((b % tables) * len(every) + a, 1), :] = row
    parts = []
    for k in range(1, groups):
        peer = lax.rem(grp + k, groups)
        parts.append(
            pltpu.make_async_remote_copy(
                src_ref=gram.at[peer],
                dst_ref=grams.at[k - 1],
                send_sem=gram_send.at[k - 1],
                recv_sem=gram_recv.at[k - 1],
                device_id={"grp": peer},
                device_id_type=MESH,
            )
        )
        parts[-1].start()
    total = gram[grp]
    for k in range(groups - 1):
        parts[k].wait_recv()
        total = total + grams[k]
    inter_ref[...] = total
    for copy in mixes + parts:
        copy.wait_send()


def lookup(n, groups, bag, ids, tables):
    count, rows, width = tables.shape
    lanes = ids.shape[1]
    pairs = count * count * groups
    chains, offsets = plan(n, count)
    hops = max(chains.values())
    dma = pltpu.SemaphoreType.DMA
    ahead = len(offsets) - 1
    return pl.pallas_call(
        functools.partial(kernel, n, groups, bag),
        out_shape=(
            jax.ShapeDtypeStruct((count, width, lanes), jnp.float32),
            jax.ShapeDtypeStruct((pairs, lanes), jnp.float32),
        ),
        in_specs=[VMEM, VMEM],
        out_specs=(VMEM, VMEM),
        scratch_shapes=[
            pltpu.VMEM((ahead, count * bag, lanes), jnp.int32),
            pltpu.VMEM((count, 2 * width, rows), jnp.bfloat16),
            pltpu.VMEM((rows // CHUNK, count * bag, lanes), jnp.float32),
            pltpu.VMEM((count, rows, lanes), jnp.bfloat16),
            pltpu.VMEM((len(chains), hops, width, lanes), jnp.float32),
            pltpu.VMEM((len(chains), hops, width, lanes), jnp.float32),
            pltpu.VMEM((groups, count, width // groups, lanes), jnp.float32),
            pltpu.VMEM((groups, pairs, lanes), jnp.float32),
            pltpu.VMEM((groups - 1, pairs, lanes), jnp.float32),
            dma((ahead,)),
            dma((ahead,)),
            dma((len(chains), hops)),
            dma((len(chains), hops)),
            dma((groups - 1,)),
            dma((groups - 1,)),
            dma((groups - 1,)),
            dma((groups - 1,)),
        ],
        compiler_params=pltpu.CompilerParams(collective_id=0, has_side_effects=True),
        name="lookup",
    )(ids, tables)


def solution(mesh):
    n, groups = mesh.shape["blk"], mesh.shape["grp"]

    def shards(tables, bag_ids):
        samples, count, bag = bag_ids.shape
        ids = bag_ids.transpose(1, 2, 0).reshape(count * bag, samples)
        pooled, inter = lookup(n, groups, bag, ids, tables)
        pooled = pooled.transpose(2, 0, 1)
        inter = inter.reshape(count, count * groups, samples).transpose(2, 0, 1)
        return pooled, inter

    return jax.shard_map(
        shards,
        mesh=mesh,
        in_specs=(P("grp", "blk", None), P("blk", "grp", None)),
        out_specs=(P("blk", "grp", None), P("blk", "grp", None)),
        check_vma=False,
    )
```

```python
import functools

import jax
import jax.numpy as jnp
from jax import lax
from jax.experimental import pallas as pl
from jax.experimental.pallas import tpu as pltpu
from jax.sharding import PartitionSpec as P

SECTIONS = 8
MESH = pl.DeviceIdType.MESH
VMEM = pl.BlockSpec(memory_space=pltpu.VMEM)
CHUNK = 256


def plan(n, tables):
    if n == SECTIONS:
        far, near = n // 2, n - 1 - n // 2
        chains = {}
        for t in range(tables):
            chains[t, 1] = far if t % 2 == 0 else near
            chains[t, -1] = near if t % 2 == 0 else far
        offsets = [far]
        for k in range(near, 0, -1):
            offsets += [k, -k]
        return chains, offsets
    chains = {(t, 1): SECTIONS - 1 for t in range(tables)}
    return chains, list(range(SECTIONS - 1, 0, -1))


def jobs_of(chains, offsets, n):
    jobs = []
    for job, offset in enumerate(offsets):
        for slot, ((t, way), hops) in enumerate(chains.items()):
            hop = hops - offset * way % n
            if hop >= 0:
                jobs.append((slot, hop, job, t))
    hops = list(chains.values())
    longest = max(hops)
    return sorted(jobs, key=lambda j: (hops[j[0]] * -1 + j[1], j[1] if j[1] < longest - 2 else -hops[j[0]]))


def kernel(n, groups, bag, ids_ref, table_ref, pooled_ref, inter_ref, *scratch):
    near_ids, table_v, table_sem, own, table_t, keys, counts, sums, held, mixed, gram, grams, *sems = scratch
    ids_send, ids_recv, ring_send, ring_recv, mix_send, mix_recv, gram_send, gram_recv = sems
    tables, rows, width = table_ref.shape
    lanes = ids_ref.shape[1]
    chunks = rows // CHUNK
    quarter = width // groups
    me, grp = lax.axis_index("blk"), lax.axis_index("grp")
    chains, offsets = plan(n, tables)
    order = list(chains)

    if n == SECTIONS:
        place = jnp.where(me % 2 == 0, me // 2, n - 1 - me // 2)
    else:
        place = me

    def at(offset):
        position = lax.rem(place + offset + n, n)
        if n == SECTIONS:
            return jnp.where(position < n // 2, 2 * position, 2 * (n - 1 - position) + 1)
        return position

    barrier = pltpu.get_barrier_semaphore()
    greeted = 0
    for offset in offsets:
        pl.semaphore_signal(barrier, inc=1, device_id={"blk": at(offset)}, device_id_type=MESH)
        greeted += 1
        if n != SECTIONS:
            pl.semaphore_signal(barrier, inc=1, device_id={"blk": at(-offset)}, device_id_type=MESH)
            greeted += 1
    for k in range(1, groups):
        pl.semaphore_signal(barrier, inc=1, device_id={"grp": lax.rem(grp + k, groups)}, device_id_type=MESH)
    fetch = pltpu.make_async_copy(table_ref, table_v, table_sem)
    fetch.start()
    pl.semaphore_wait(barrier, greeted + groups - 1)

    asks = []
    for job, offset in enumerate(offsets):
        asks.append(
            pltpu.make_async_remote_copy(
                src_ref=ids_ref,
                dst_ref=near_ids.at[job],
                send_sem=ids_send.at[job],
                recv_sem=ids_recv.at[job],
                device_id={"blk": at(-offset)},
                device_id_type=MESH,
            )
        )
        asks[-1].start()

    fetch.wait()
    for t in range(tables):
        flipped = table_v[t].T
        high = flipped.astype(jnp.bfloat16)
        table_t[t, pl.ds(0, width), :] = high
        table_t[t, pl.ds(width, width), :] = (flipped - high.astype(jnp.float32)).astype(jnp.bfloat16)
    index = lax.broadcasted_iota(jnp.int32, (CHUNK, lanes), 0).astype(jnp.float32).astype(jnp.bfloat16)
    one, zero = jnp.bfloat16(1), jnp.bfloat16(0)

    def partial_sum(codes, section, t):
        local = jnp.where((codes & (SECTIONS - 1)) == section, codes >> 3, -1)
        for c in range(chunks):
            inside = (local >= c * CHUNK) & (local < (c + 1) * CHUNK)
            keys[c] = jnp.where(inside, local - c * CHUNK, 2 * CHUNK).astype(jnp.float32)

        def unit(c, carry):
            total = jnp.zeros((CHUNK, lanes), jnp.bfloat16)
            for p in range(bag):
                key = jnp.broadcast_to(keys[c, pl.ds(p, 1), :], (CHUNK, lanes))
                total = total + jnp.where(index == key.astype(jnp.bfloat16), one, zero)
            counts[pl.ds(pl.multiple_of(c * CHUNK, CHUNK), CHUNK), :] = total
            return carry

        lax.fori_loop(0, chunks, unit, 0, unroll=2 if chunks % 2 == 0 else 1)
        both = jnp.dot(table_t[t], counts[...], preferred_element_type=jnp.float32)
        return both[:width] + both[width:]

    for t in range(tables):
        own[t] = partial_sum(ids_ref[pl.ds(t * bag, bag), :], 0, t)

    flying = {}
    arrived = set()
    for slot, hop, job, t in jobs_of(chains, offsets, n):
        way = order[slot][1]
        if job not in arrived:
            asks[job].wait_recv()
            arrived.add(job)
        section = lax.rem(at(offsets[job]) + n - me, n)
        total = partial_sum(near_ids[job, pl.ds(t * bag, bag), :], section, t)
        if hop > 0:
            flying[slot, hop - 1].wait_recv()
            total = total + held[slot, hop - 1]
        sums[slot, hop] = total
        flying[slot, hop] = pltpu.make_async_remote_copy(
            src_ref=sums.at[slot, hop],
            dst_ref=held.at[slot, hop],
            send_sem=ring_send.at[slot, hop],
            recv_sem=ring_recv.at[slot, hop],
            device_id={"blk": at(way)},
            device_id_type=MESH,
        )
        flying[slot, hop].start()
    for slot, (t, way) in enumerate(order):
        last = chains[t, way] - 1
        flying[slot, last].wait_recv()
        own[t] = own[t] + held[slot, last]

    mixes = []
    for k in range(1, groups):
        peer = lax.rem(grp + k, groups)
        mixes.append(
            pltpu.make_async_remote_copy(
                src_ref=own.at[:, pl.ds(pl.multiple_of(peer * quarter, quarter), quarter)],
                dst_ref=mixed.at[grp],
                send_sem=mix_send.at[k - 1],
                recv_sem=mix_recv.at[k - 1],
                device_id={"grp": peer},
                device_id_type=MESH,
            )
        )
        mixes[-1].start()
    mixed[grp] = own[:, pl.ds(pl.multiple_of(grp * quarter, quarter), quarter)]
    for t in range(tables):
        pooled_ref[pl.ds(t, lanes, stride=tables), :] = own[t].T
    for copy in list(flying.values()) + asks:
        copy.wait_send()
    for copy in mixes:
        copy.wait_recv()
    every = [mixed[g, t] for g in range(groups) for t in range(tables)]
    for a in range(len(every)):
        for b in range(a, len(every)):
            row = jnp.sum(every[a] * every[b], axis=0, keepdims=True) / width
            gram[a // tables, pl.ds((a % tables) * len(every) + b, 1), :] = row
            if a != b:
                gram[b // tables, pl.ds((b % tables) * len(every) + a, 1), :] = row
    parts = []
    for k in range(1, groups):
        peer = lax.rem(grp + k, groups)
        parts.append(
            pltpu.make_async_remote_copy(
                src_ref=gram.at[peer],
                dst_ref=grams.at[k - 1],
                send_sem=gram_send.at[k - 1],
                recv_sem=gram_recv.at[k - 1],
                device_id={"grp": peer},
                device_id_type=MESH,
            )
        )
        parts[-1].start()
    total = gram[grp]
    for k in range(groups - 1):
        parts[k].wait_recv()
        total = total + grams[k]
    inter_ref[...] = total
    for copy in mixes + parts:
        copy.wait_send()


def lookup(n, groups, bag, ids, tables):
    count, rows, width = tables.shape
    lanes = ids.shape[1]
    pairs = count * count * groups
    chains, offsets = plan(n, count)
    hops = max(chains.values())
    dma = pltpu.SemaphoreType.DMA
    ahead = len(offsets)
    return pl.pallas_call(
        functools.partial(kernel, n, groups, bag),
        out_shape=(
            jax.ShapeDtypeStruct((lanes * count, width), jnp.float32),
            jax.ShapeDtypeStruct((pairs, lanes), jnp.float32),
        ),
        in_specs=[VMEM, pl.BlockSpec(memory_space=pl.ANY)],
        out_specs=(VMEM, VMEM),
        scratch_shapes=[
            pltpu.VMEM((ahead, count * bag, lanes), jnp.int32),
            pltpu.VMEM((count, rows, width), jnp.float32),
            pltpu.SemaphoreType.DMA,
            pltpu.VMEM((count, width, lanes), jnp.float32),
            pltpu.VMEM((count, 2 * width, rows), jnp.bfloat16),
            pltpu.VMEM((rows // CHUNK, bag, lanes), jnp.float32),
            pltpu.VMEM((rows, lanes), jnp.bfloat16),
            pltpu.VMEM((len(chains), hops, width, lanes), jnp.float32),
            pltpu.VMEM((len(chains), hops, width, lanes), jnp.float32),
            pltpu.VMEM((groups, count, width // groups, lanes), jnp.float32),
            pltpu.VMEM((groups, pairs, lanes), jnp.float32),
            pltpu.VMEM((groups - 1, pairs, lanes), jnp.float32),
            dma((ahead,)),
            dma((ahead,)),
            dma((len(chains), hops)),
            dma((len(chains), hops)),
            dma((groups - 1,)),
            dma((groups - 1,)),
            dma((groups - 1,)),
            dma((groups - 1,)),
        ],
        compiler_params=pltpu.CompilerParams(collective_id=0, has_side_effects=True),
        name="lookup",
    )(ids, tables)


def solution(mesh):
    n, groups = mesh.shape["blk"], mesh.shape["grp"]

    def shards(tables, bag_ids):
        samples, count, bag = bag_ids.shape
        ids = bag_ids.transpose(1, 2, 0).reshape(count * bag, samples)
        pooled, inter = lookup(n, groups, bag, ids, tables)
        pooled = pooled.reshape(samples, count, tables.shape[2])
        inter = inter.reshape(count, count * groups, samples).transpose(2, 0, 1)
        return pooled, inter

    return jax.shard_map(
        shards,
        mesh=mesh,
        in_specs=(P("grp", "blk", None), P("blk", "grp", None)),
        out_specs=(P("blk", "grp", None), P("blk", "grp", None)),
        check_vma=False,
    )
```
